32 devices in a mesh: group: 8 (over z, y), expert: 4 (over x, core).
Axes of the slice: x: 2, y: 2, z: 4, core: 2. Of those that a mesh axis runs over, the one named last changes fastest.
Arguments:
- train_inputs: float32 [32, 16, 1024], P(('group', 'expert')), as said below
- inv_factor: float32 [32, 1024, 1024], P(('group', 'expert')), as said below
- weights: float32 [32, 1024, 512], P(('group', 'expert')), as said below
- candidates: float32 [16, 4096], replicated, as said below
- test_ids: int32 [1024], replicated, may hold values from 0 to 4095
- basis: bfloat16 [512, 32768], P(None, ('group', 'expert')), may hold values from -0.25 to 0.25
- climatology: float32 [32768], P(('group', 'expert')), may hold values from -3 to 3
Outputs:
- field: bfloat16 [1024, 32768], P(None, ('group', 'expert'))
The draws below stay inside these ranges and needn't reach their ends.
Inputs may be any that keep to these rules, and one draw needn't show every extreme that they name: inv_factor[e] is lower triangular with L L^T = K + 0.1 I inverted, where K[r, s] = exp(-0.5 |x_r - x_s|^2) over the columns of train_inputs[e]. `train_inputs`: entries of magnitude below 2. `candidates`: entries of magnitude below 2. `weights`: entries of magnitude at most 0.6 * sqrt(32).
All inputs are finite; a program needn't handle non-finite values.
Results may differ from the reference program's by a relative error of at most 0.0045.
Values may be sent and summed in bfloat16 or wider, within the bound.
No kernel may reach another device: no remote copies, remote signals or barrier semaphores. Data moves between devices by JAX's collectives and lax.ppermute only.
A program may use at most 64 MiB of HBM per device.

```python
import math
import jax
import jax.numpy as jnp
from jax import lax

DIN = 16
RUNS = 1024
OUT = 512
TESTS = 1024
CANDS = 4096
CELL_DEV = 1024
EXPERTS = 32
CELLS = 32768


noise_var = 0.1


def shared_offset(key):
    return jax.random.uniform(jax.random.fold_in(key, 101), (DIN,), jnp.float32, -0.25, 0.25)


def draw_train_inputs(key, part):
    offset = shared_offset(key)
    half_width = math.sqrt(12.0 / DIN)
    spread = jax.random.uniform(jax.random.fold_in(key, 102), (EXPERTS, DIN, RUNS), jnp.float32, -half_width, half_width)
    return offset[None, :, None] + spread


def draw_inv_factor(key, part):
    train_points = draw_train_inputs(key, part)
    identity = jnp.eye(RUNS, dtype=jnp.float32)

    def factor_one(points):
        squares = jnp.sum(points * points, axis=0)
        inner = jnp.dot(points.T, points, precision=lax.Precision.HIGHEST)
        gram = jnp.exp(-0.5 * (squares[:, None] + squares[None, :] - 2.0 * inner))
        gram = 0.5 * (gram + gram.T) + noise_var * identity
        lower = jnp.linalg.cholesky(gram)
        return jax.scipy.linalg.solve_triangular(lower, identity, lower=True)
    return lax.map(factor_one, train_points)


def draw_weights(key, part):
    scale = 0.2 * math.sqrt(EXPERTS)
    values = jax.random.normal(jax.random.fold_in(key, 106), (EXPERTS, RUNS, OUT), jnp.float32)
    return jnp.clip(values, -3.0, 3.0) * scale


def draw_candidates(key, part):
    offset = shared_offset(key)
    half_width = math.sqrt(12.0 / DIN)
    spread = jax.random.uniform(jax.random.fold_in(key, 104), (DIN, CANDS), jnp.float32, -half_width, half_width)
    return offset[:, None] + spread


def place_ends(values, stream_key, smallest, top_value):
    longest = values.shape.index(max(values.shape))
    spots = []
    for shift in (0, 1):
        where = [jax.random.randint(jax.random.fold_in(stream_key, axis), (), 0, length) for axis, length in enumerate(values.shape)]
        where[longest] = (where[longest] + shift) % values.shape[longest]
        spots.append(tuple(where))
    return values.at[spots[0]].set(smallest).at[spots[1]].set(top_value)


def levels(stream_key, shape, split, smallest, largest):
    def one(dim, shards_of):
        heights = jax.random.uniform(jax.random.fold_in(jax.random.fold_in(stream_key, 6), dim), (shards_of,), jnp.float32, smallest / len(split), largest / len(split))
        return jnp.repeat(jnp.exp(heights), shape[dim] // shards_of).reshape((-1,) + (1,) * (len(shape) - dim - 1))

    loudness = one(*split[0])
    for cut in split[1:]:
        loudness = loudness * one(*cut)
    return loudness


def noise(stream_key, dims, width, most, pieces=(), held_as=jnp.bfloat16):
    result = width * jax.random.normal(stream_key, dims, jnp.float32)
    if pieces:
        result = result * levels(stream_key, dims, pieces, -0.22, 0.18)
    return jnp.clip(result, -most, most).astype(held_as)


def setup_inputs(seed: int = 0) -> dict:
    key_list = jax.random.split(jax.random.key(seed), 8)
    return {
        "train_inputs": draw_train_inputs(jax.random.fold_in(key_list[7], 71), 0),
        "inv_factor": draw_inv_factor(jax.random.fold_in(key_list[7], 71), 0),
        "weights": draw_weights(jax.random.fold_in(key_list[7], 71), 0),
        "candidates": draw_candidates(jax.random.fold_in(key_list[7], 71), 0),
        "test_ids": place_ends(jax.random.randint(key_list[4], (TESTS,), 0, CANDS), jax.random.fold_in(key_list[4], 1), 0, CANDS - 1).astype(jnp.int32),
        "basis": noise(key_list[5], (OUT, CELLS), OUT ** -0.5, 0.25, ((1, 32),)),
        "climatology": noise(key_list[6], (CELLS,), 0.5, 3.0, ((0, 32),), jnp.float32),
    }


signal_var = 1.0
noise_var = 0.1

def cross_cov(train_points, query_points):
    sq_train = jnp.sum(train_points * train_points, axis=0)
    sq_query = jnp.sum(query_points * query_points, axis=0)
    inner = lax.dot_general(train_points.astype(jnp.float32), query_points.astype(jnp.float32), (((0,), (0,)), ((), ())), precision=lax.Precision.HIGHEST, preferred_element_type=jnp.float32)
    return signal_var * jnp.exp(-0.5 * (sq_train[:, None] + sq_query[None, :] - 2.0 * inner))

def expert_terms(train_points, factor, expert_weights, query_points):
    cross_kernel = cross_cov(train_points, query_points)
    expert_mean = lax.dot_general(cross_kernel.astype(jnp.float32), expert_weights.astype(jnp.float32), (((0,), (0,)), ((), ())), precision=lax.Precision.HIGHEST, preferred_element_type=jnp.float32)
    whitened = jnp.dot(factor.astype(jnp.float32), cross_kernel.astype(jnp.float32), precision=lax.Precision.HIGHEST, preferred_element_type=jnp.float32)
    explained = jnp.sum(whitened * whitened, axis=0)
    prior_var = signal_var + noise_var
    post_var = prior_var - explained
    beta_weight = 0.5 * (jnp.log(prior_var) - jnp.log(post_var))
    precision_term = beta_weight / post_var
    return (expert_mean * precision_term[:, None], precision_term, beta_weight)

def reference(train_inputs, inv_factor, weights, candidates, test_ids, basis, climatology):
    query_points = jnp.take(candidates, test_ids.astype(jnp.int32), axis=1)

    def accumulate(carry, items):
        partial_value, weight_term, beta_weight = expert_terms(items[0], items[1], items[2], query_points)
        return ((carry[0] + partial_value, carry[1] + weight_term, carry[2] + beta_weight), None)
    start = (jnp.zeros((TESTS, OUT), jnp.float32), jnp.zeros((TESTS,), jnp.float32), jnp.zeros((TESTS,), jnp.float32))
    sums, _ = lax.scan(accumulate, start, (train_inputs, inv_factor, weights))
    mean_total, weight_total, beta_total = sums
    precision = weight_total + (1.0 - beta_total) / (signal_var + noise_var)
    coefficients = (mean_total / precision[:, None]).astype(jnp.bfloat16)
    nblocks = CELLS // CELL_DEV
    basis_blocks = basis.reshape(OUT, nblocks, CELL_DEV).transpose(1, 0, 2)
    clim_blocks = climatology.reshape(nblocks, CELL_DEV)

    def reconstruct(items):
        field_sum = jnp.dot(coefficients.astype(jnp.float32), items[0].astype(jnp.float32), preferred_element_type=jnp.float32) + items[1][None, :]
        return field_sum.astype(jnp.bfloat16)
    blocks = lax.map(reconstruct, (basis_blocks, clim_blocks))
    return blocks.transpose(1, 0, 2).reshape(TESTS, CELLS)
```

```python
import jax
import jax.numpy as jnp
from jax import lax
from jax.experimental import pallas as pl
from jax.experimental.pallas import tpu as pltpu
from jax.sharding import PartitionSpec as P

signal_var = 1.0
noise_var = 0.1
prior_var = signal_var + noise_var

AXES = ("group", "expert")
LANES = 128
EXTRA = 8
F32 = jnp.float32
BF16 = jnp.bfloat16


def split3(v):
    a = v.astype(BF16).astype(F32)
    b = (v - a).astype(BF16).astype(F32)
    c = ((v - a) - b).astype(BF16).astype(F32)
    return a, b, c


def row_iota(shape):
    return lax.broadcasted_iota(jnp.int32, shape, 0)


def pick_rows(rows, count, width):
    at = row_iota((count, width))
    out = jnp.zeros((count, width), F32)
    for i, row in enumerate(rows):
        out = jnp.where(at == i, row, out)
    return out


def column_to_row(col):
    return jnp.transpose(jnp.broadcast_to(col, (LANES, LANES)))[0:1, :]


def row_to_column(row):
    return jnp.transpose(jnp.broadcast_to(row, (LANES, LANES)))


def experts_kernel(where, ids, cand, train, inv, wts, send, keep, inv_s, w_s, x_s, k1_s, k2_s, sem):
    runs = train.shape[2]
    dims = train.shape[1]
    out = wts.shape[2]
    rows = k1_s.shape[0]
    blocks = rows // LANES
    tri = 256
    nt = runs // tri
    copies = []
    for j in range(nt):
        region = (pl.ds(j * tri, tri), pl.ds(0, (j + 1) * tri))
        copies.append(pltpu.make_async_copy(inv.at[(0,) + region], inv_s.at[region], sem.at[j]))
    copies.append(pltpu.make_async_copy(wts.at[0], w_s, sem.at[nt]))
    for copy in copies:
        copy.start()

    x = train[0]
    x1, x2, x3 = split3(x)
    s1, s2, s3 = split3(-0.5 * jnp.sum(x * x, axis=0, keepdims=True))
    one = jnp.ones((1, runs), F32)
    tail = pick_rows((s1, s2, s3, one, one, one), 8, runs)
    pad = jnp.zeros((LANES - 6 * dims - 8, runs), F32)
    x_s[...] = jnp.concatenate((x1, x2, x1, x2, x3, x1, tail, pad), axis=0).astype(BF16)

    groups = cand.shape[1] // LANES
    for b in range(blocks):
        own = b // (blocks // 2)
        quarter = blocks // 2
        block = where[0] * blocks + jnp.where(own == 1, where[1], 1 - where[1]) * quarter + b % quarter
        ident = ids[block]
        low = jnp.broadcast_to(ident & (LANES - 1), (dims, LANES))
        high = jnp.broadcast_to(ident // LANES, (dims, LANES))
        q = jnp.zeros((dims, LANES), F32)
        for g in range(groups):
            part = jnp.take_along_axis(
                cand[:, g * LANES : (g + 1) * LANES], low, axis=1, mode="promise_in_bounds"
            )
            q = jnp.where(high == g, part, q)
        q1, q2, q3 = split3(q)
        t1, t2, t3 = split3(-0.5 * jnp.sum(q * q, axis=0, keepdims=True))
        unit = jnp.ones((1, LANES), F32)
        side = pick_rows((unit, unit, unit, t1, t2, t3), 8, LANES)
        rest = jnp.zeros((LANES - 6 * dims - 8, LANES), F32)
        stacked = jnp.concatenate((q1, q1, q2, q2, q1, q3, side, rest), axis=0)
        lhs = jnp.transpose(stacked).astype(BF16)
        expo = jnp.dot(lhs, x_s[...], preferred_element_type=F32)
        kern = signal_var * jnp.exp(expo)
        k1 = kern.astype(BF16)
        at = pl.ds(b * LANES, LANES)
        k1_s[at, :] = k1
        k2_s[at, :] = (kern - k1.astype(F32)).astype(BF16)

    nt_dims = (((1,), (1,)), ((), ()))
    total = jnp.zeros((rows, LANES), F32)
    for j in range(nt):
        copies[j].wait()
        depth = (j + 1) * tri
        a = inv_s[j * tri : depth, :depth]
        a1 = a.astype(BF16)
        a2 = (a - a1.astype(F32)).astype(BF16)
        k1 = k1_s[:, :depth]
        k2 = k2_s[:, :depth]
        white = (
            lax.dot_general(k1, a1, nt_dims, preferred_element_type=F32)
            + lax.dot_general(k2, a1, nt_dims, preferred_element_type=F32)
            + lax.dot_general(k1, a2, nt_dims, preferred_element_type=F32)
        )
        square = white * white
        for i in range(tri // LANES):
            total = total + square[:, i * LANES : (i + 1) * LANES]
    explained = jnp.sum(total, axis=1, keepdims=True)
    post = prior_var - explained
    beta = 0.5 * (jnp.log(prior_var) - jnp.log(post))
    prec = beta / post
    share = prec - beta * (1.0 / prior_var)

    copies[nt].wait()
    w = w_s[...]
    w1 = w.astype(BF16)
    w2 = (w - w1.astype(F32)).astype(BF16)
    k1 = k1_s[...]
    mean = (
        jnp.dot(k1, w1, preferred_element_type=F32)
        + jnp.dot(k2_s[...], w1, preferred_element_type=F32)
        + jnp.dot(k1, w2, preferred_element_type=F32)
    )
    value = mean * prec
    half = rows // 2
    share_rows = [column_to_row(share[b * LANES : (b + 1) * LANES, :]) for b in range(blocks)]
    zeros = [jnp.zeros((1, out - half), F32)] if out > half else []
    row_send = jnp.concatenate(share_rows[: blocks // 2] + zeros, axis=1)
    row_keep = jnp.concatenate(share_rows[blocks // 2 :] + zeros, axis=1)
    send[:half, :] = value[:half].astype(BF16)
    send[half:, :] = message_rows(row_send)
    keep[:half, :] = value[half:]
    keep[half:, :] = pick_rows((row_keep,), EXTRA, out)


def message_rows(row):
    high = row.astype(BF16).astype(F32)
    return pick_rows((high, row - high), EXTRA, row.shape[1]).astype(BF16)


def expert_half(where, ids, cand, train, inv, wts):
    runs, out = wts.shape[1], wts.shape[2]
    rows = ids.shape[0] * LANES // 2
    vmem = pl.BlockSpec(memory_space=pltpu.VMEM)
    hbm = pl.BlockSpec(memory_space=pl.ANY)
    shape = (rows // 2 + EXTRA, out)
    return pl.pallas_call(
        experts_kernel,
        in_specs=[pl.BlockSpec(memory_space=pltpu.SMEM), vmem, vmem, vmem, hbm, hbm],
        out_specs=[vmem, vmem],
        out_shape=[jax.ShapeDtypeStruct(shape, BF16), jax.ShapeDtypeStruct(shape, F32)],
        scratch_shapes=[
            pltpu.VMEM((runs, runs), F32),
            pltpu.VMEM((runs, out), F32),
            pltpu.VMEM((LANES, runs), BF16),
            pltpu.VMEM((rows, runs), BF16),
            pltpu.VMEM((rows, runs), BF16),
            pltpu.SemaphoreType.DMA((runs // 256 + 1,)),
        ],
        cost_estimate=pl.CostEstimate(
            flops=6 * rows * runs * (runs + out), transcendentals=rows * runs, bytes_accessed=8 * runs * runs
        ),
        name="experts",
    )(where, ids, cand, train, inv, wts)


def add_parts(parts):
    keep = parts[0]
    rows = keep.shape[0] - EXTRA
    data = keep[:rows, :]
    row = keep[rows : rows + 1, :]
    for ref in parts[1:]:
        data = data + ref[:rows, :].astype(F32)
        low = ref[rows:, :].astype(F32)
        row = row + (low[0:1, :] + low[1:2, :])
    return data, row


def send_kernel(keep, recv, send):
    rows = keep.shape[0] - EXTRA
    data, row = add_parts((keep, recv))
    send[:rows, :] = data.astype(BF16)
    send[rows:, :] = message_rows(row)


def split_kernel(where, *refs):
    parts, (send, keep, data_s) = refs[:-3], refs[-3:]
    data, row = add_parts(parts)
    data_s[...] = data
    rows = send.shape[0] - EXTRA
    width = row.shape[1]
    mine = where[0]
    first = row[:, :rows]
    second = row[:, rows : 2 * rows]
    fill = [jnp.zeros((1, width - rows), F32)]
    row_keep = jnp.concatenate([jnp.where(mine == 0, first, second)] + fill, axis=1)
    row_send = jnp.concatenate([jnp.where(mine == 0, second, first)] + fill, axis=1)
    send[:rows, :] = data_s[pl.ds((1 - mine) * rows, rows), :].astype(BF16)
    send[rows:, :] = message_rows(row_send)
    keep[:rows, :] = data_s[pl.ds(mine * rows, rows), :]
    keep[rows:, :] = pick_rows((row_keep,), EXTRA, width)


def both_kernel(keep, recv, send, keep_out):
    rows = keep.shape[0] - EXTRA
    data, row = add_parts((keep, recv))
    send[:rows, :] = data.astype(BF16)
    send[rows:, :] = message_rows(row)
    keep_out[:rows, :] = data
    keep_out[rows:, :] = pick_rows((row,), EXTRA, row.shape[1])


def divide_kernel(keep, recv, coef):
    data, row = add_parts((keep, recv))
    total = row + 1.0 / prior_var
    for b in range(coef.shape[0] // LANES):
        at = slice(b * LANES, (b + 1) * LANES)
        column = row_to_column(total[:, at])[:, 0:1]
        coef[at, :] = (data[at] / column).astype(BF16)


def vmem_call(kernel, outs, *args, smem=0, scratch=(), name=None):
    vmem = pl.BlockSpec(memory_space=pltpu.VMEM)
    specs = [pl.BlockSpec(memory_space=pltpu.SMEM)] * smem + [vmem] * (len(args) - smem)
    return pl.pallas_call(
        kernel,
        in_specs=specs,
        out_specs=[vmem] * len(outs),
        out_shape=[jax.ShapeDtypeStruct(s, d) for s, d in outs],
        scratch_shapes=list(scratch),
        name=name,
    )(*args)


def make_field_kernel(count, aliased):
    def kernel(where, basis, clim, *refs):
        coefs = refs[:count]
        out, buf, sem = refs[-3:]
        copies = []
        at = 0
        for i, coef in enumerate(coefs):
            rows = coef.shape[0]
            acc = jnp.dot(coef[...], basis[...], preferred_element_type=F32)
            buf[at : at + rows, :] = (acc + clim[...]).astype(BF16)
            start = pl.multiple_of(where[i], 8)
            copy = pltpu.make_async_copy(buf.at[pl.ds(at, rows)], out.at[pl.ds(start, rows)], sem.at[i])
            copy.start()
            copies.append(copy)
            at += rows
        for copy in copies:
            copy.wait()

    return kernel


def field_rows(starts, basis, clim, coefs, tests, out=None):
    vmem = pl.BlockSpec(memory_space=pltpu.VMEM)
    hbm = pl.BlockSpec(memory_space=pl.ANY)
    cells = basis.shape[1]
    rows = sum(c.shape[0] for c in coefs)
    args = [jnp.stack(starts), basis, clim, *coefs]
    specs = [pl.BlockSpec(memory_space=pltpu.SMEM)] + [vmem] * (len(args) - 1)
    alias = {}
    if out is not None:
        alias = {len(args): 0}
        args.append(out)
        specs.append(hbm)
    return pl.pallas_call(
        make_field_kernel(len(coefs), out is not None),
        in_specs=specs,
        out_specs=hbm,
        out_shape=jax.ShapeDtypeStruct((tests, cells), BF16),
        input_output_aliases=alias,
        scratch_shapes=[pltpu.VMEM((rows, cells), BF16), pltpu.SemaphoreType.DMA((len(coefs),))],
        cost_estimate=pl.CostEstimate(
            flops=2 * rows * basis.shape[0] * cells, transcendentals=0, bytes_accessed=2 * rows * cells
        ),
        name="field",
    )(*args)


def solution(mesh):
    n_group, n_expert = mesh.shape["group"], mesh.shape["expert"]
    assert n_group & (n_group - 1) == 0 and n_expert & (n_expert - 1) == 0
    assert n_group >= 2 and n_expert >= 4

    def swap(value, group_mask, expert_mask):
        pairs = []
        for g in range(n_group):
            for e in range(n_expert):
                pairs.append((g * n_expert + e, (g ^ group_mask) * n_expert + (e ^ expert_mask)))
        return lax.ppermute(value, AXES, pairs)

    core = (0, 1)
    far = (0, 2)
    near = (1, 0)
    adding = []
    for bit in range(2, n_expert.bit_length() - 1):
        adding.append((0, 1 << bit))
    for bit in range(1, n_group.bit_length() - 1):
        adding.append(((1 << (bit + 1)) - 2, 0))

    def body(train_inputs, inv_factor, weights, candidates, test_ids, basis, climatology):
        tests = test_ids.shape[0]
        out = weights.shape[2]
        block = tests // 8
        expert = lax.axis_index("expert")
        group = lax.axis_index("group")
        c = expert & 1
        x = (expert >> 1) & 1
        y = group & 1
        ids = test_ids.reshape(tests // LANES, 1, LANES)
        first = jnp.stack([1 - x, c]).astype(jnp.int32)
        second = jnp.stack([x, c]).astype(jnp.int32)

        send, keep = expert_half(first, ids, candidates, train_inputs, inv_factor, weights)
        got = swap(send, *core)
        big = (2 * block + EXTRA, out)
        (send_x,) = vmem_call(send_kernel, [(big, BF16)], keep, got, name="sum_core")
        got_x = swap(send_x, *far)
        send, keep = expert_half(second, ids, candidates, train_inputs, inv_factor, weights)
        got = swap(send, *core)
        small = (block + EXTRA, out)
        where_y = jnp.stack([y]).astype(jnp.int32)
        send, keep = vmem_call(
            split_kernel,
            [(small, BF16), (small, F32)],
            where_y,
            keep,
            got,
            got_x,
            smem=1,
            scratch=[pltpu.VMEM((2 * block, out), F32)],
            name="sum_x",
        )
        got = swap(send, *near)
        for mask in adding:
            send, keep = vmem_call(both_kernel, [(small, BF16), (small, F32)], keep, got, name="sum_more")
            got = swap(send, *mask)
        (coef,) = vmem_call(divide_kernel, [((block, out), BF16)], keep, got, name="coefficients")

        clim = climatology.reshape(1, -1)
        half = block // 2

        def start(xx, cc, yy):
            return ((xx * 4 + cc * 2 + yy) * block).astype(jnp.int32)

        by_x = swap(coef, *far)
        by_y = swap(coef, *near)
        diag_a = swap(by_x[:half], *near)
        diag_b = swap(by_y[half:], *far)
        others = [swap(v, *core) for v in (coef, by_x, by_y)]
        nx, ny, nc = 1 - x, 1 - y, 1 - c
        field = field_rows([start(x, c, y), start(nx, c, y), start(x, c, ny)], basis, clim, [coef, by_x, by_y], tests)
        field = field_rows([start(x, nc, y), start(nx, nc, y), start(x, nc, ny)], basis, clim, others, tests, field)
        last = [swap(v, *core) for v in (diag_a, diag_b)]
        diag = start(nx, c, ny)
        diag_other = start(nx, nc, ny)
        field = field_rows([diag, diag + half], basis, clim, [diag_a, diag_b], tests, field)
        return field_rows([diag_other, diag_other + half], basis, clim, last, tests, field)

    return jax.shard_map(
        body,
        mesh=mesh,
        in_specs=(
            P(AXES, None, None),
            P(AXES, None, None),
            P(AXES, None, None),
            P(),
            P(),
            P(None, AXES),
            P(AXES),
        ),
        out_specs=P(None, AXES),
        check_vma=False,
    )
```

```python
import jax
import jax.numpy as jnp
from jax import lax
from jax.experimental import pallas as pl
from jax.experimental.pallas import tpu as pltpu
from jax.sharding import PartitionSpec as P


signal_var = 1.0
noise_var = 0.1
prior_var = signal_var + noise_var

AXES = ("group", "expert")
LANES = 128
EXTRA = 8
F32 = jnp.float32
BF16 = jnp.bfloat16


def split3(v):
    a = v.astype(BF16).astype(F32)
    b = (v - a).astype(BF16).astype(F32)
    c = ((v - a) - b).astype(BF16).astype(F32)
    return a, b, c


def row_iota(shape):
    return lax.broadcasted_iota(jnp.int32, shape, 0)


def pick_rows(rows, count, width):
    at = row_iota((count, width))
    out = jnp.zeros((count, width), F32)
    for i, row in enumerate(rows):
        out = jnp.where(at == i, row, out)
    return out


def column_to_row(col):
    return jnp.transpose(jnp.broadcast_to(col, (LANES, LANES)))[0:1, :]


def row_to_column(row):
    return jnp.transpose(jnp.broadcast_to(row, (LANES, LANES)))


def place():
    expert = lax.axis_index("expert")
    group = lax.axis_index("group")
    return (expert >> 1) & 1, expert & 1, group & 1


def make_experts_kernel(near_half):
    def kernel(ids, cand, train, inv, wts, send, keep, ids_s, cand_s, train_s, inv_s, w_s, x_s, k1_s, k2_s, sem):
        runs = train.shape[2]
        dims = train.shape[1]
        out = wts.shape[2]
        rows = k1_s.shape[0]
        blocks = rows // LANES
        tri = 256
        nt = runs // tri
        small = [
            pltpu.make_async_copy(train.at[0], train_s, sem.at[0]),
            pltpu.make_async_copy(ids, ids_s, sem.at[1]),
            pltpu.make_async_copy(cand, cand_s, sem.at[2]),
        ]
        big = [pltpu.make_async_copy(wts.at[0], w_s, sem.at[3])]
        for j in reversed(range(nt)):
            region = (pl.ds(j * tri, tri), pl.ds(0, (j + 1) * tri))
            big.append(pltpu.make_async_copy(inv.at[(0,) + region], inv_s.at[region], sem.at[4 + j]))
        for copy in small + big:
            copy.start()
        at_x, at_core, _ = place()
        at_half = at_x if near_half else 1 - at_x

        small[0].wait()
        x = train_s[...]
        x1, x2, x3 = split3(x)
        s1, s2, s3 = split3(-0.5 * jnp.sum(x * x, axis=0, keepdims=True))
        one = jnp.ones((1, runs), F32)
        tail = pick_rows((s1, s2, s3, one, one, one), 8, runs)
        pad = jnp.zeros((LANES - 6 * dims - 8, runs), F32)
        x_s[...] = jnp.concatenate((x1, x2, x1, x2, x3, x1, tail, pad), axis=0).astype(BF16)

        small[1].wait()
        small[2].wait()
        groups = cand.shape[1] // LANES
        quarter = blocks // 2
        for b in range(blocks):
            at_quarter = at_core if b >= quarter else 1 - at_core
            ident = ids_s[at_half * blocks + at_quarter * quarter + b % quarter]
            low = jnp.broadcast_to(ident & (LANES - 1), (dims, LANES))
            high = jnp.broadcast_to(ident // LANES, (dims, LANES))
            q = jnp.zeros((dims, LANES), F32)
            for g in range(groups):
                part = jnp.take_along_axis(
                    cand_s[:, g * LANES : (g + 1) * LANES], low, axis=1, mode="promise_in_bounds"
                )
                q = jnp.where(high == g, part, q)
            q1, q2, q3 = split3(q)
            t1, t2, t3 = split3(-0.5 * jnp.sum(q * q, axis=0, keepdims=True))
            unit = jnp.ones((1, LANES), F32)
            side = pick_rows((unit, unit, unit, t1, t2, t3), 8, LANES)
            rest = jnp.zeros((LANES - 6 * dims - 8, LANES), F32)
            stacked = jnp.concatenate((q1, q1, q2, q2, q1, q3, side, rest), axis=0)
            lhs = jnp.transpose(stacked).astype(BF16)
            expo = jnp.dot(lhs, x_s[...], preferred_element_type=F32)
            kern = signal_var * jnp.exp(expo)
            k1 = kern.astype(BF16)
            at = pl.ds(b * LANES, LANES)
            k1_s[at, :] = k1
            k2_s[at, :] = (kern - k1.astype(F32)).astype(BF16)

        for copy in big:
            copy.wait()
        total = jnp.zeros((rows, LANES), F32)
        means = []
        nt_dims = (((1,), (1,)), ((), ()))
        for j in reversed(range(nt)):
            depth = (j + 1) * tri
            a = inv_s[j * tri : depth, :depth]
            a1 = a.astype(BF16)
            a2 = (a - a1.astype(F32)).astype(BF16)
            white = (
                lax.dot_general(k1_s[:, :depth], a1, nt_dims, preferred_element_type=F32)
                + lax.dot_general(k2_s[:, :depth], a1, nt_dims, preferred_element_type=F32)
                + lax.dot_general(k1_s[:, :depth], a2, nt_dims, preferred_element_type=F32)
            )
            square = white * white
            for i in range(tri // LANES):
                total = total + square[:, i * LANES : (i + 1) * LANES]
            if len(means) * tri < out:
                w = w_s[:, len(means) * tri : (len(means) + 1) * tri]
                w1 = w.astype(BF16)
                w2 = (w - w1.astype(F32)).astype(BF16)
                means.append(
                    jnp.dot(k1_s[...], w1, preferred_element_type=F32)
                    + jnp.dot(k2_s[...], w1, preferred_element_type=F32)
                    + jnp.dot(k1_s[...], w2, preferred_element_type=F32)
                )
        explained = jnp.sum(total, axis=1, keepdims=True)
        post = prior_var - explained
        beta = 0.5 * (jnp.log(prior_var) - jnp.log(post))
        prec = beta / post
        share = prec - beta * (1.0 / prior_var)

        half = rows // 2
        for i, mean in enumerate(means):
            cols = slice(i * tri, (i + 1) * tri)
            value = mean * prec
            send[:half, cols] = value[:half].astype(BF16)
            keep[:half, cols] = value[half:]
        share_rows = [column_to_row(share[b * LANES : (b + 1) * LANES, :]) for b in range(blocks)]
        zeros = [jnp.zeros((1, out - half), F32)] if out > half else []
        row_send = jnp.concatenate(share_rows[:quarter] + zeros, axis=1)
        row_keep = jnp.concatenate(share_rows[quarter:] + zeros, axis=1)
        send[half:, :] = message_rows(row_send)
        keep[half:, :] = pick_rows((row_keep,), EXTRA, out)

    return kernel


def message_rows(row):
    high = row.astype(BF16).astype(F32)
    return pick_rows((high, row - high), EXTRA, row.shape[1]).astype(BF16)


def in_vmem(value):
    return pltpu.with_memory_space_constraint(value, pltpu.VMEM)


def expert_half(near_half, ids, cand, train, inv, wts):
    dims, runs, out = train.shape[1], wts.shape[1], wts.shape[2]
    rows = ids.shape[0] * LANES // 2
    vmem = pl.BlockSpec(memory_space=pltpu.VMEM)
    hbm = pl.BlockSpec(memory_space=pl.ANY)
    shape = (rows // 2 + EXTRA, out)
    return pl.pallas_call(
        make_experts_kernel(near_half),
        in_specs=[hbm] * 5,
        out_specs=[vmem, vmem],
        out_shape=[pltpu.VMEM(shape, BF16), pltpu.VMEM(shape, F32)],
        scratch_shapes=[
            pltpu.VMEM(ids.shape, jnp.int32),
            pltpu.VMEM(cand.shape, F32),
            pltpu.VMEM((dims, runs), F32),
            pltpu.VMEM((runs, runs), F32),
            pltpu.VMEM((runs, out), F32),
            pltpu.VMEM((LANES, runs), BF16),
            pltpu.VMEM((rows, runs), BF16),
            pltpu.VMEM((rows, runs), BF16),
            pltpu.SemaphoreType.DMA((4 + runs // 256,)),
        ],
        cost_estimate=pl.CostEstimate(
            flops=6 * rows * runs * (runs + out), transcendentals=rows * runs, bytes_accessed=8 * runs * runs
        ),
        name="experts_near" if near_half else "experts_far",
    )(ids, cand, train, inv, wts)


def add_parts(parts):
    keep = parts[0]
    rows = keep.shape[0] - EXTRA
    data = keep[:rows, :]
    row = keep[rows : rows + 1, :]
    for ref in parts[1:]:
        data = data + ref[:rows, :].astype(F32)
        low = ref[rows:, :].astype(F32)
        row = row + (low[0:1, :] + low[1:2, :])
    return data, row


def send_kernel(keep, recv, send):
    rows = keep.shape[0] - EXTRA
    data, row = add_parts((keep, recv))
    send[:rows, :] = data.astype(BF16)
    send[rows:, :] = message_rows(row)


def split_kernel(*refs):
    parts, (send, keep, data_s) = refs[:-3], refs[-3:]
    data, row = add_parts(parts)
    data_s[...] = data
    rows = send.shape[0] - EXTRA
    width = row.shape[1]
    _, _, mine = place()
    first = row[:, :rows]
    second = row[:, rows : 2 * rows]
    fill = [jnp.zeros((1, width - rows), F32)]
    row_keep = jnp.concatenate([jnp.where(mine == 0, first, second)] + fill, axis=1)
    row_send = jnp.concatenate([jnp.where(mine == 0, second, first)] + fill, axis=1)
    send[:rows, :] = data_s[pl.ds((1 - mine) * rows, rows), :].astype(BF16)
    send[rows:, :] = message_rows(row_send)
    keep[:rows, :] = data_s[pl.ds(mine * rows, rows), :]
    keep[rows:, :] = pick_rows((row_keep,), EXTRA, width)


def both_kernel(keep, recv, send, keep_out):
    rows = keep.shape[0] - EXTRA
    data, row = add_parts((keep, recv))
    send[:rows, :] = data.astype(BF16)
    send[rows:, :] = message_rows(row)
    keep_out[:rows, :] = data
    keep_out[rows:, :] = pick_rows((row,), EXTRA, row.shape[1])


def divide_kernel(keep, recv, coef):
    data, row = add_parts((keep, recv))
    total = row + 1.0 / prior_var
    for b in range(coef.shape[0] // LANES):
        at = slice(b * LANES, (b + 1) * LANES)
        column = row_to_column(total[:, at])[:, 0:1]
        coef[at, :] = (data[at] / column).astype(BF16)


def vmem_call(kernel, outs, *args, scratch=()):
    vmem = pl.BlockSpec(memory_space=pltpu.VMEM)
    return pl.pallas_call(
        kernel,
        in_specs=[vmem] * len(args),
        out_specs=[vmem] * len(outs),
        out_shape=[pltpu.VMEM(s, d) for s, d in outs],
        scratch_shapes=list(scratch),
    )(*[in_vmem(a) for a in args])


def make_field_kernel(places):
    def kernel(basis, clim, *refs):
        coefs = refs[: len(places)]
        out, buf, sem = refs[-3:]
        here = place()
        block = out.shape[0] // 8
        copies = []
        at = 0
        for i, (coef, (flips, offset)) in enumerate(zip(coefs, places)):
            rows = coef.shape[0]
            acc = jnp.dot(coef[...], basis[...], preferred_element_type=F32)
            buf[at : at + rows, :] = (acc + clim[...]).astype(BF16)
            bx, bc, by = [1 - h if f else h for h, f in zip(here, flips)]
            start = pl.multiple_of((bx * 4 + bc * 2 + by) * block + offset, rows)
            copy = pltpu.make_async_copy(buf.at[pl.ds(at, rows)], out.at[pl.ds(start, rows)], sem.at[i])
            copy.start()
            copies.append(copy)
            at += rows
        for copy in copies:
            copy.wait()

    return kernel


def field_rows(parts, basis, clim, tests, out=None):
    vmem = pl.BlockSpec(memory_space=pltpu.VMEM)
    hbm = pl.BlockSpec(memory_space=pl.ANY)
    cells = basis.shape[1]
    rows = sum(c.shape[0] for c, _, _ in parts)
    args = [in_vmem(v) for v in [basis, clim] + [c for c, _, _ in parts]]
    specs = [vmem] * len(args)
    alias = {}
    if out is not None:
        alias = {len(args): 0}
        args.append(out)
        specs.append(hbm)
    return pl.pallas_call(
        make_field_kernel([(flips, offset) for _, flips, offset in parts]),
        in_specs=specs,
        out_specs=hbm,
        out_shape=jax.ShapeDtypeStruct((tests, cells), BF16),
        input_output_aliases=alias,
        scratch_shapes=[pltpu.VMEM((rows, cells), BF16), pltpu.SemaphoreType.DMA((len(parts),))],
        cost_estimate=pl.CostEstimate(
            flops=2 * rows * basis.shape[0] * cells, transcendentals=0, bytes_accessed=2 * rows * cells
        ),
        name="field",
    )(*args)


def solution(mesh):
    n_group, n_expert = mesh.shape["group"], mesh.shape["expert"]
    assert n_group & (n_group - 1) == 0 and n_expert & (n_expert - 1) == 0
    assert n_group >= 2 and n_expert >= 4

    def swap(value, group_mask, expert_mask):
        pairs = []
        for g in range(n_group):
            for e in range(n_expert):
                pairs.append((g * n_expert + e, (g ^ group_mask) * n_expert + (e ^ expert_mask)))
        return lax.ppermute(value, AXES, pairs)

    core = (0, 1)
    far = (0, 2)
    near = (1, 0)
    adding = []
    for bit in range(2, n_expert.bit_length() - 1):
        adding.append((0, 1 << bit))
    for bit in range(1, n_group.bit_length() - 1):
        adding.append(((1 << (bit + 1)) - 2, 0))

    def work(train_inputs, inv_factor, weights, candidates, test_ids, basis, climatology):
        tests = test_ids.shape[0]
        out = weights.shape[2]
        block = tests // 8
        ids = test_ids.reshape(tests // LANES, 1, LANES)
        big = (2 * block + EXTRA, out)
        small = (block + EXTRA, out)

        send, keep = expert_half(False, ids, candidates, train_inputs, inv_factor, weights)
        got = swap(send, *core)
        (send,) = vmem_call(send_kernel, [(big, BF16)], keep, got)
        send, ids = lax.optimization_barrier((send, ids))
        got_x = swap(send, *far)
        send, keep = expert_half(True, ids, candidates, train_inputs, inv_factor, weights)
        got = swap(send, *core)
        send, keep = vmem_call(
            split_kernel, [(small, BF16), (small, F32)], keep, got, got_x, scratch=[pltpu.VMEM((2 * block, out), F32)]
        )
        got = swap(send, *near)
        for mask in adding:
            send, keep = vmem_call(both_kernel, [(small, BF16), (small, F32)], keep, got)
            got = swap(send, *mask)
        (coef,) = vmem_call(divide_kernel, [((block, out), BF16)], keep, got)

        clim = climatology.reshape(1, -1)
        half = block // 2
        by_x = swap(coef, *far)
        by_y = swap(coef, *near)
        by_c = swap(coef, *core)
        field = field_rows([(coef, (0, 0, 0), 0)], basis, clim, tests)
        diag_a = swap(by_x[:half], *near)
        diag_b = swap(by_y[half:], *far)
        by_cx = swap(by_x, *core)
        by_cy = swap(by_y, *core)
        field = field_rows(
            [(by_c, (0, 1, 0), 0), (by_x, (1, 0, 0), 0), (by_y, (0, 0, 1), 0)], basis, clim, tests, field
        )
        diag_ca = swap(diag_a, *core)
        diag_cb = swap(diag_b, *core)
        field = field_rows(
            [
                (by_cx, (1, 1, 0), 0),
                (by_cy, (0, 1, 1), 0),
                (diag_a, (1, 0, 1), 0),
                (diag_b, (1, 0, 1), half),
            ],
            basis,
            clim,
            tests,
            field,
        )
        return field_rows([(diag_ca, (1, 1, 1), 0), (diag_cb, (1, 1, 1), half)], basis, clim, tests, field)

    return jax.shard_map(
        work,
        mesh=mesh,
        in_specs=(
            P(AXES, None, None),
            P(AXES, None, None),
            P(AXES, None, None),
            P(),
            P(),
            P(None, AXES),
            P(AXES),
        ),
        out_specs=P(None, AXES),
        check_vma=False,
    )
```

```python
import jax
import jax.numpy as jnp
from jax import lax
from jax.experimental import pallas as pl
from jax.experimental.pallas import tpu as pltpu
from jax.sharding import PartitionSpec as P


signal_var = 1.0
noise_var = 0.1
prior_var = signal_var + noise_var

AXES = ("group", "expert")
LANES = 128
EXTRA = 8
F32 = jnp.float32
BF16 = jnp.bfloat16


def split3(v):
    a = v.astype(BF16).astype(F32)
    b = (v - a).astype(BF16).astype(F32)
    c = ((v - a) - b).astype(BF16).astype(F32)
    return a, b, c


def row_iota(shape):
    return lax.broadcasted_iota(jnp.int32, shape, 0)


def pick_rows(rows, count, width):
    at = row_iota((count, width))
    out = jnp.zeros((count, width), F32)
    for i, row in enumerate(rows):
        out = jnp.where(at == i, row, out)
    return out


def column_to_row(col):
    return jnp.transpose(jnp.broadcast_to(col, (LANES, LANES)))[0:1, :]


def row_to_column(row):
    return jnp.transpose(jnp.broadcast_to(row, (LANES, LANES)))


def place():
    expert = lax.axis_index("expert")
    group = lax.axis_index("group")
    return (expert >> 1) & 1, expert & 1, group & 1


def make_experts_kernel(near_half):
    def kernel(ids, cand, train, inv, wts, send, keep, ids_s, cand_s, train_s, inv_s, w_s, x_s, k1_s, k2_s, sem):
        runs = train.shape[2]
        dims = train.shape[1]
        out = wts.shape[2]
        rows = k1_s.shape[0]
        blocks = rows // LANES
        tri = 256
        nt = runs // tri
        small = [
            pltpu.make_async_copy(train.at[0], train_s, sem.at[0]),
            pltpu.make_async_copy(ids, ids_s, sem.at[1]),
            pltpu.make_async_copy(cand, cand_s, sem.at[2]),
        ]
        big = [pltpu.make_async_copy(wts.at[0], w_s, sem.at[3])]
        for j in reversed(range(nt)):
            region = (pl.ds(j * tri, tri), pl.ds(0, (j + 1) * tri))
            big.append(pltpu.make_async_copy(inv.at[(0,) + region], inv_s.at[region], sem.at[4 + j]))
        for copy in small + big:
            copy.start()
        at_x, at_core, _ = place()
        at_half = at_x if near_half else 1 - at_x

        small[0].wait()
        x = train_s[...]
        x1, x2, x3 = split3(x)
        s1, s2, s3 = split3(-0.5 * jnp.sum(x * x, axis=0, keepdims=True))
        one = jnp.ones((1, runs), F32)
        tail = pick_rows((s1, s2, s3, one, one, one), 8, runs)
        pad = jnp.zeros((LANES - 6 * dims - 8, runs), F32)
        x_s[...] = jnp.concatenate((x1, x2, x1, x2, x3, x1, tail, pad), axis=0).astype(BF16)

        small[1].wait()
        small[2].wait()
        groups = cand.shape[1] // LANES
        quarter = blocks // 2
        for b in range(blocks):
            at_quarter = at_core if b >= quarter else 1 - at_core
            ident = ids_s[at_half * blocks + at_quarter * quarter + b % quarter]
            low = jnp.broadcast_to(ident & (LANES - 1), (dims, LANES))
            high = jnp.broadcast_to(ident // LANES, (dims, LANES))
            q = jnp.zeros((dims, LANES), F32)
            for g in range(groups):
                part = jnp.take_along_axis(
                    cand_s[:, g * LANES : (g + 1) * LANES], low, axis=1, mode="promise_in_bounds"
                )
                q = jnp.where(high == g, part, q)
            q1, q2, q3 = split3(q)
            t1, t2, t3 = split3(-0.5 * jnp.sum(q * q, axis=0, keepdims=True))
            unit = jnp.ones((1, LANES), F32)
            side = pick_rows((unit, unit, unit, t1, t2, t3), 8, LANES)
            rest = jnp.zeros((LANES - 6 * dims - 8, LANES), F32)
            stacked = jnp.concatenate((q1, q1, q2, q2, q1, q3, side, rest), axis=0)
            lhs = jnp.transpose(stacked).astype(BF16)
            expo = jnp.dot(lhs, x_s[...], preferred_element_type=F32)
            kern = signal_var * jnp.exp(expo)
            k1 = kern.astype(BF16)
            at = pl.ds(b * LANES, LANES)
            k1_s[at, :] = k1
            k2_s[at, :] = (kern - k1.astype(F32)).astype(BF16)

        for copy in big:
            copy.wait()
        total = jnp.zeros((rows, LANES), F32)
        means = []
        nt_dims = (((1,), (1,)), ((), ()))
        for j in reversed(range(nt)):
            depth = (j + 1) * tri
            a = inv_s[j * tri : depth, :depth]
            a1 = a.astype(BF16)
            a2 = (a - a1.astype(F32)).astype(BF16)
            white = (
                lax.dot_general(k1_s[:, :depth], a1, nt_dims, preferred_element_type=F32)
                + lax.dot_general(k2_s[:, :depth], a1, nt_dims, preferred_element_type=F32)
                + lax.dot_general(k1_s[:, :depth], a2, nt_dims, preferred_element_type=F32)
            )
            square = white * white
            for i in range(tri // LANES):
                total = total + square[:, i * LANES : (i + 1) * LANES]
            if len(means) * tri < out:
                w = w_s[:, len(means) * tri : (len(means) + 1) * tri]
                w1 = w.astype(BF16)
                w2 = (w - w1.astype(F32)).astype(BF16)
                means.append(
                    jnp.dot(k1_s[...], w1, preferred_element_type=F32)
                    + jnp.dot(k2_s[...], w1, preferred_element_type=F32)
                    + jnp.dot(k1_s[...], w2, preferred_element_type=F32)
                )
        explained = jnp.sum(total, axis=1, keepdims=True)
        post = prior_var - explained
        beta = 0.5 * (jnp.log(prior_var) - jnp.log(post))
        prec = beta / post
        share = prec - beta * (1.0 / prior_var)

        half = rows // 2
        for i, mean in enumerate(means):
            cols = slice(i * tri, (i + 1) * tri)
            value = mean * prec
            send[:half, cols] = value[:half].astype(BF16)
            keep[:half, cols] = value[half:]
        share_rows = [column_to_row(share[b * LANES : (b + 1) * LANES, :]) for b in range(blocks)]
        zeros = [jnp.zeros((1, out - half), F32)] if out > half else []
        row_send = jnp.concatenate(share_rows[:quarter] + zeros, axis=1)
        row_keep = jnp.concatenate(share_rows[quarter:] + zeros, axis=1)
        send[half:, :] = message_rows(row_send)
        keep[half:, :] = pick_rows((row_keep,), EXTRA, out)

    return kernel


def message_rows(row):
    high = row.astype(BF16).astype(F32)
    return pick_rows((high, row - high), EXTRA, row.shape[1]).astype(BF16)


def in_vmem(value):
    return pltpu.with_memory_space_constraint(value, pltpu.VMEM)


def expert_half(near_half, ids, cand, train, inv, wts):
    dims, runs, out = train.shape[1], wts.shape[1], wts.shape[2]
    rows = ids.shape[0] * LANES // 2
    vmem = pl.BlockSpec(memory_space=pltpu.VMEM)
    hbm = pl.BlockSpec(memory_space=pl.ANY)
    shape = (rows // 2 + EXTRA, out)
    return pl.pallas_call(
        make_experts_kernel(near_half),
        in_specs=[hbm] * 5,
        out_specs=[vmem, vmem],
        out_shape=[pltpu.VMEM(shape, BF16), pltpu.VMEM(shape, F32)],
        scratch_shapes=[
            pltpu.VMEM(ids.shape, jnp.int32),
            pltpu.VMEM(cand.shape, F32),
            pltpu.VMEM((dims, runs), F32),
            pltpu.VMEM((runs, runs), F32),
            pltpu.VMEM((runs, out), F32),
            pltpu.VMEM((LANES, runs), BF16),
            pltpu.VMEM((rows, runs), BF16),
            pltpu.VMEM((rows, runs), BF16),
            pltpu.SemaphoreType.DMA((4 + runs // 256,)),
        ],
        cost_estimate=pl.CostEstimate(
            flops=6 * rows * runs * (runs + out), transcendentals=rows * runs, bytes_accessed=8 * runs * runs
        ),
        name="experts_near" if near_half else "experts_far",
    )(ids, cand, train, inv, wts)


def add_parts(parts):
    keep = parts[0]
    rows = keep.shape[0] - EXTRA
    data = keep[:rows, :]
    row = keep[rows : rows + 1, :]
    for ref in parts[1:]:
        data = data + ref[:rows, :].astype(F32)
        low = ref[rows:, :].astype(F32)
        row = row + (low[0:1, :] + low[1:2, :])
    return data, row


def send_kernel(keep, recv, send):
    rows = keep.shape[0] - EXTRA
    data, row = add_parts((keep, recv))
    send[:rows, :] = data.astype(BF16)
    send[rows:, :] = message_rows(row)


def split_kernel(*refs):
    parts, (send, same, keep, data_s) = refs[:-4], refs[-4:]
    data, row = add_parts(parts)
    data_s[...] = data
    rows = send.shape[0] - EXTRA
    width = row.shape[1]
    _, _, mine = place()
    first = row[:, :rows]
    second = row[:, rows : 2 * rows]
    fill = [jnp.zeros((1, width - rows), F32)]
    row_keep = jnp.concatenate([jnp.where(mine == 0, first, second)] + fill, axis=1)
    row_send = jnp.concatenate([jnp.where(mine == 0, second, first)] + fill, axis=1)
    send[:rows, :] = data_s[pl.ds((1 - mine) * rows, rows), :].astype(BF16)
    send[rows:, :] = message_rows(row_send)
    kept = data_s[pl.ds(mine * rows, rows), :]
    keep[:rows, :] = kept
    keep[rows:, :] = pick_rows((row_keep,), EXTRA, width)
    same[:rows, :] = kept.astype(BF16)
    same[rows:, :] = message_rows(row_keep)


def both_kernel(*refs):
    parts, (send, keep_out) = refs[:-2], refs[-2:]
    rows = keep_out.shape[0] - EXTRA
    data, row = add_parts(parts)
    send[:rows, :] = data.astype(BF16)
    send[rows:, :] = message_rows(row)
    keep_out[:rows, :] = data
    keep_out[rows:, :] = pick_rows((row,), EXTRA, row.shape[1])


def divide_kernel(*refs):
    coef = refs[-1]
    data, row = add_parts(refs[:-1])
    total = row + 1.0 / prior_var
    for b in range(coef.shape[0] // LANES):
        at = slice(b * LANES, (b + 1) * LANES)
        column = row_to_column(total[:, at])[:, 0:1]
        coef[at, :] = (data[at] / column).astype(BF16)


def vmem_call(kernel, outs, *args, scratch=()):
    vmem = pl.BlockSpec(memory_space=pltpu.VMEM)
    return pl.pallas_call(
        kernel,
        in_specs=[vmem] * len(args),
        out_specs=[vmem] * len(outs),
        out_shape=[pltpu.VMEM(s, d) for s, d in outs],
        scratch_shapes=list(scratch),
    )(*[in_vmem(a) for a in args])


def make_field_kernel(places):
    def kernel(basis, clim, *refs):
        coefs = refs[: len(places)]
        out, buf, sem = refs[-3:]
        here = place()
        block = out.shape[0] // 8
        copies = []
        at = 0
        for i, (coef, (flips, offset)) in enumerate(zip(coefs, places)):
            rows = coef.shape[0]
            acc = jnp.dot(coef[...], basis[...], preferred_element_type=F32)
            buf[at : at + rows, :] = (acc + clim[...]).astype(BF16)
            bx, bc, by = [1 - h if f else h for h, f in zip(here, flips)]
            start = pl.multiple_of((bx * 4 + bc * 2 + by) * block + offset, rows)
            copy = pltpu.make_async_copy(buf.at[pl.ds(at, rows)], out.at[pl.ds(start, rows)], sem.at[i])
            copy.start()
            copies.append(copy)
            at += rows
        for copy in copies:
            copy.wait()

    return kernel


def field_rows(parts, basis, clim, tests, out=None):
    vmem = pl.BlockSpec(memory_space=pltpu.VMEM)
    hbm = pl.BlockSpec(memory_space=pl.ANY)
    cells = basis.shape[1]
    rows = sum(c.shape[0] for c, _, _ in parts)
    args = [in_vmem(v) for v in [basis, clim] + [c for c, _, _ in parts]]
    specs = [vmem] * len(args)
    alias = {}
    if out is not None:
        alias = {len(args): 0}
        args.append(out)
        specs.append(hbm)
    return pl.pallas_call(
        make_field_kernel([(flips, offset) for _, flips, offset in parts]),
        in_specs=specs,
        out_specs=hbm,
        out_shape=jax.ShapeDtypeStruct((tests, cells), BF16),
        input_output_aliases=alias,
        scratch_shapes=[pltpu.VMEM((rows, cells), BF16), pltpu.SemaphoreType.DMA((len(parts),))],
        cost_estimate=pl.CostEstimate(
            flops=2 * rows * basis.shape[0] * cells, transcendentals=0, bytes_accessed=2 * rows * cells
        ),
        name="field",
    )(*args)


def solution(mesh):
    n_group, n_expert = mesh.shape["group"], mesh.shape["expert"]
    assert n_group & (n_group - 1) == 0 and n_expert & (n_expert - 1) == 0
    assert n_group >= 2 and n_expert >= 4

    def swap(value, group_mask, expert_mask):
        pairs = []
        for g in range(n_group):
            for e in range(n_expert):
                pairs.append((g * n_expert + e, (g ^ group_mask) * n_expert + (e ^ expert_mask)))
        return lax.ppermute(value, AXES, pairs)

    def both_masks(a, b):
        return a[0] ^ b[0], a[1] ^ b[1]

    core = (0, 1)
    far = (0, 2)
    near = (1, 0)
    adding = []
    for bit in range(2, n_expert.bit_length() - 1):
        adding.append((0, 1 << bit))
    for bit in range(1, n_group.bit_length() - 1):
        adding.append(((1 << (bit + 1)) - 2, 0))

    def work(train_inputs, inv_factor, weights, candidates, test_ids, basis, climatology):
        tests = test_ids.shape[0]
        out = weights.shape[2]
        block = tests // 8
        ids = test_ids.reshape(tests // LANES, 1, LANES)
        big = (2 * block + EXTRA, out)
        small = (block + EXTRA, out)

        send, keep = expert_half(False, ids, candidates, train_inputs, inv_factor, weights)
        got = swap(send, *core)
        (send,) = vmem_call(send_kernel, [(big, BF16)], keep, got)
        send, ids = lax.optimization_barrier((send, ids))
        got_x = swap(send, *far)
        send, keep = expert_half(True, ids, candidates, train_inputs, inv_factor, weights)
        got = swap(send, *core)
        send, same, keep = vmem_call(
            split_kernel,
            [(small, BF16), (small, BF16), (small, F32)],
            keep,
            got,
            got_x,
            scratch=[pltpu.VMEM((2 * block, out), F32)],
        )
        got_d = swap(send, *both_masks(near, adding[0]))
        got_y = swap(send, *near)
        got_z = swap(same, *adding[0])
        parts = [keep, got_y, got_z, got_d]
        for mask in adding[1:]:
            send, keep = vmem_call(both_kernel, [(small, BF16), (small, F32)], *parts)
            parts = [keep, swap(send, *mask)]
        (coef,) = vmem_call(divide_kernel, [((block, out), BF16)], *parts)

        clim = climatology.reshape(1, -1)
        by_d = swap(coef, *both_masks(far, near))
        by_x = swap(coef, *far)
        by_y = swap(coef, *near)
        by_c = swap(coef, *core)
        field = field_rows([(coef, (0, 0, 0), 0), (by_c, (0, 1, 0), 0)], basis, clim, tests)
        by_cx = swap(by_x, *core)
        by_cy = swap(by_y, *core)
        field = field_rows([(by_x, (1, 0, 0), 0), (by_y, (0, 0, 1), 0)], basis, clim, tests, field)
        by_cd = swap(by_d, *core)
        parts = [(by_cx, (1, 1, 0), 0), (by_cy, (0, 1, 1), 0), (by_d, (1, 0, 1), 0)]
        field = field_rows(parts, basis, clim, tests, field)
        return field_rows([(by_cd, (1, 1, 1), 0)], basis, clim, tests, field)

    return jax.shard_map(
        work,
        mesh=mesh,
        in_specs=(
            P(AXES, None, None),
            P(AXES, None, None),
            P(AXES, None, None),
            P(),
            P(),
            P(None, AXES),
            P(AXES),
        ),
        out_specs=P(None, AXES),
        check_vma=False,
    )
```

```python
import jax
import jax.numpy as jnp
from jax import lax
from jax.experimental import pallas as pl
from jax.experimental.pallas import tpu as pltpu
from jax.sharding import PartitionSpec as P


signal_var = 1.0
noise_var = 0.1
prior_var = signal_var + noise_var

AXES = ("group", "expert")
LANES = 128
LEAVING = ((1, 1), (1, 0), (0, 1))
STAYING = ((0, 0),)
TRI = 256
VMEM_LIMIT = 32 * 1024 * 1024
EXTRA = 8
F32 = jnp.float32
BF16 = jnp.bfloat16


def split3(v):
    a = v.astype(BF16).astype(F32)
    b = (v - a).astype(BF16).astype(F32)
    c = ((v - a) - b).astype(BF16).astype(F32)
    return a, b, c


def row_iota(shape):
    return lax.broadcasted_iota(jnp.int32, shape, 0)


def pick_rows(rows, count, width):
    at = row_iota((count, width))
    out = jnp.zeros((count, width), F32)
    for i, row in enumerate(rows):
        out = jnp.where(at == i, row, out)
    return out


def column_to_row(col):
    return jnp.transpose(jnp.broadcast_to(col, (LANES, LANES)))[0:1, :]


def row_to_column(row):
    return jnp.transpose(jnp.broadcast_to(row, (LANES, LANES)))


def place():
    expert = lax.axis_index("expert")
    group = lax.axis_index("group")
    return (expert >> 1) & 1, expert & 1, group & 1


def gathered(ident, cand):
    dims = cand.shape[0]
    low = jnp.broadcast_to(ident & (LANES - 1), (dims, LANES))
    high = jnp.broadcast_to(ident // LANES, (dims, LANES))
    q = jnp.zeros((dims, LANES), F32)
    for g in range(cand.shape[1] // LANES):
        part = jnp.take_along_axis(cand[:, g * LANES : (g + 1) * LANES], low, axis=1, mode="promise_in_bounds")
        q = jnp.where(high == g, part, q)
    return q


def query_side(q):
    dims = q.shape[0]
    q1, q2, q3 = split3(q)
    t1, t2, t3 = split3(-0.5 * jnp.sum(q * q, axis=0, keepdims=True))
    unit = jnp.ones((1, LANES), F32)
    side = pick_rows((unit, unit, unit, t1, t2, t3), 8, LANES)
    rest = jnp.zeros((LANES - 6 * dims - 8, LANES), F32)
    return jnp.transpose(jnp.concatenate((q1, q1, q2, q2, q1, q3, side, rest), axis=0)).astype(BF16)


def train_side(x):
    dims, runs = x.shape
    x1, x2, x3 = split3(x)
    s1, s2, s3 = split3(-0.5 * jnp.sum(x * x, axis=0, keepdims=True))
    one = jnp.ones((1, runs), F32)
    tail = pick_rows((s1, s2, s3, one, one, one), 8, runs)
    pad = jnp.zeros((LANES - 6 * dims - 8, runs), F32)
    return jnp.concatenate((x1, x2, x1, x2, x3, x1, tail, pad), axis=0).astype(BF16)


def fill_kernels(flips, ids, cand, x_ref, k1_s, k2_s):
    at_x, at_core, at_y = place()
    for b in range(k1_s.shape[0] // LANES):
        flip_x, flip_y = flips[b % len(flips)]
        x = 1 - at_x if flip_x else at_x
        y = 1 - at_y if flip_y else at_y
        c = at_core if b >= len(flips) else 1 - at_core
        lhs = query_side(gathered(ids[x * 4 + c * 2 + y], cand))
        kern = signal_var * jnp.exp(jnp.dot(lhs, x_ref[...], preferred_element_type=F32))
        k1 = kern.astype(BF16)
        at = pl.ds(b * LANES, LANES)
        k1_s[at, :] = k1
        k2_s[at, :] = (kern - k1.astype(F32)).astype(BF16)


def experts_terms(inv_parts, wts_parts, k1_s, k2_s, out, send, keep):
    rows, runs = k1_s.shape
    total = jnp.zeros((rows, LANES), F32)
    means = []
    nt_dims = (((1,), (1,)), ((), ()))
    for j in reversed(range(runs // TRI)):
        depth = (j + 1) * TRI
        a1, a2 = inv_parts(j)
        white = (
            lax.dot_general(k1_s[:, :depth], a1, nt_dims, preferred_element_type=F32)
            + lax.dot_general(k2_s[:, :depth], a1, nt_dims, preferred_element_type=F32)
            + lax.dot_general(k1_s[:, :depth], a2, nt_dims, preferred_element_type=F32)
        )
        square = white * white
        for i in range(TRI // LANES):
            total = total + square[:, i * LANES : (i + 1) * LANES]
        if len(means) * TRI < out:
            w = wts_parts(slice(len(means) * TRI, (len(means) + 1) * TRI))
            mean = jnp.dot(k1_s[...], w[0], preferred_element_type=F32)
            if len(w) > 1:
                mean = mean + jnp.dot(k2_s[...], w[0], preferred_element_type=F32)
                mean = mean + jnp.dot(k1_s[...], w[1], preferred_element_type=F32)
            means.append(mean)
    explained = jnp.sum(total, axis=1, keepdims=True)
    post = prior_var - explained
    beta = 0.5 * (jnp.log(prior_var) - jnp.log(post))
    prec = beta / post
    share = prec - beta * (1.0 / prior_var)

    half = rows // 2
    for i, mean in enumerate(means):
        cols = slice(i * TRI, (i + 1) * TRI)
        value = mean * prec
        send[:half, cols] = value[:half].astype(BF16)
        keep[:half, cols] = value[half:]
    blocks = rows // LANES
    share_rows = [column_to_row(share[b * LANES : (b + 1) * LANES, :]) for b in range(blocks)]
    zeros = [jnp.zeros((1, out - half), F32)] if out > half else []
    row_send = jnp.concatenate(share_rows[: blocks // 2] + zeros, axis=1)
    row_keep = jnp.concatenate(share_rows[blocks // 2 :] + zeros, axis=1)
    send[half:, :] = message_rows(row_send)
    keep[half:, :] = pick_rows((row_keep,), EXTRA, out)


def far_kernel(ids, cand, train, inv, wts, send, keep, x_o, a1_o, a2_o, w1_o, w2_o, *scratch):
    ids_s, cand_s, train_s, inv_s, w_s, k1_s, k2_s, sem = scratch
    runs, out = wts.shape[1], wts.shape[2]
    small = [
        pltpu.make_async_copy(train.at[0], train_s, sem.at[0]),
        pltpu.make_async_copy(ids, ids_s, sem.at[1]),
        pltpu.make_async_copy(cand, cand_s, sem.at[2]),
    ]
    big = [pltpu.make_async_copy(wts.at[0], w_s, sem.at[3])]
    for j in reversed(range(runs // TRI)):
        region = (pl.ds(j * TRI, TRI), pl.ds(0, (j + 1) * TRI))
        big.append(pltpu.make_async_copy(inv.at[(0,) + region], inv_s.at[region], sem.at[4 + j]))
    for copy in small + big:
        copy.start()
    small[0].wait()
    x_o[...] = train_side(train_s[...])
    small[1].wait()
    small[2].wait()
    fill_kernels(LEAVING, ids_s, cand_s, x_o, k1_s, k2_s)
    for copy in big:
        copy.wait()

    def inv_parts(j):
        depth = (j + 1) * TRI
        region = (slice(j * TRI, depth), slice(0, depth))
        a = inv_s[region]
        a1 = a.astype(BF16)
        a2 = (a - a1.astype(F32)).astype(BF16)
        a1_o[region] = a1
        a2_o[region] = a2
        return a1, a2

    def wts_parts(cols):
        w = w_s[:, cols]
        w1 = w.astype(BF16)
        w1_o[:, cols] = w1
        w2_o[:, cols] = (w - w1.astype(F32)).astype(BF16)
        return (w1,)

    experts_terms(inv_parts, wts_parts, k1_s, k2_s, out, send, keep)


def near_kernel(ids, cand, x_r, a1_r, a2_r, w1_r, w2_r, send, keep, k1_s, k2_s):
    fill_kernels(STAYING, ids, cand, x_r, k1_s, k2_s)

    def inv_parts(j):
        region = (slice(j * TRI, (j + 1) * TRI), slice(0, (j + 1) * TRI))
        return a1_r[region], a2_r[region]

    experts_terms(inv_parts, lambda cols: (w1_r[:, cols], w2_r[:, cols]), k1_s, k2_s, w1_r.shape[1], send, keep)


def message_rows(row):
    high = row.astype(BF16).astype(F32)
    return pick_rows((high, row - high), EXTRA, row.shape[1]).astype(BF16)


def in_vmem(value):
    return pltpu.with_memory_space_constraint(value, pltpu.VMEM)


def far_half(ids, cand, train, inv, wts):
    dims, runs, out = train.shape[1], wts.shape[1], wts.shape[2]
    rows = 2 * len(LEAVING) * LANES
    vmem = pl.BlockSpec(memory_space=pltpu.VMEM)
    hbm = pl.BlockSpec(memory_space=pltpu.HBM)
    shape = (rows // 2 + EXTRA, out)
    return pl.pallas_call(
        far_kernel,
        in_specs=[hbm] * 5,
        out_specs=[vmem] * 7,
        out_shape=[
            pltpu.VMEM(shape, BF16),
            pltpu.VMEM(shape, F32),
            pltpu.VMEM((LANES, runs), BF16),
            pltpu.VMEM((runs, runs), BF16),
            pltpu.VMEM((runs, runs), BF16),
            pltpu.VMEM((runs, out), BF16),
            pltpu.VMEM((runs, out), BF16),
        ],
        scratch_shapes=[
            pltpu.VMEM(ids.shape, jnp.int32),
            pltpu.VMEM(cand.shape, F32),
            pltpu.VMEM((dims, runs), F32),
            pltpu.VMEM((runs, runs), F32),
            pltpu.VMEM((runs, out), F32),
            pltpu.VMEM((rows, runs), BF16),
            pltpu.VMEM((rows, runs), BF16),
            pltpu.SemaphoreType.DMA((4 + runs // TRI,)),
        ],
        compiler_params=pltpu.CompilerParams(vmem_limit_bytes=VMEM_LIMIT),
        name="experts_far",
    )(*[in_hbm(v) for v in (ids, cand, train, inv, wts)])


def near_half(ids, cand, x_parts, inv1, inv2, wts1, wts2):
    runs, out = wts1.shape
    rows = 2 * len(STAYING) * LANES
    vmem = pl.BlockSpec(memory_space=pltpu.VMEM)
    shape = (rows // 2 + EXTRA, out)
    return pl.pallas_call(
        near_kernel,
        in_specs=[vmem] * 7,
        out_specs=[vmem] * 2,
        out_shape=[pltpu.VMEM(shape, BF16), pltpu.VMEM(shape, F32)],
        scratch_shapes=[pltpu.VMEM((rows, runs), BF16), pltpu.VMEM((rows, runs), BF16)],
        compiler_params=pltpu.CompilerParams(vmem_limit_bytes=VMEM_LIMIT),
        name="experts_near",
    )(*[in_vmem(v) for v in (ids, cand, x_parts, inv1, inv2, wts1, wts2)])


def add_parts(parts):
    keep = parts[0]
    rows = keep.shape[0] - EXTRA
    data = keep[:rows, :]
    row = keep[rows : rows + 1, :]
    for ref in parts[1:]:
        data = data + ref[:rows, :].astype(F32)
        low = ref[rows:, :].astype(F32)
        row = row + (low[0:1, :] + low[1:2, :])
    return data, row


def leave_kernel(keep, recv, *sends):
    data, row = add_parts((keep, recv))
    width = row.shape[1]
    for i, send in enumerate(sends):
        rows = send.shape[0] - EXTRA
        at = slice(i * rows, (i + 1) * rows)
        send[:rows, :] = data[at].astype(BF16)
        send[rows:, :] = message_rows(jnp.concatenate((row[:, at], jnp.zeros((1, width - rows), F32)), axis=1))


def both_kernel(*refs):
    parts, (send, keep_out) = refs[:-2], refs[-2:]
    rows = keep_out.shape[0] - EXTRA
    data, row = add_parts(parts)
    send[:rows, :] = data.astype(BF16)
    send[rows:, :] = message_rows(row)
    keep_out[:rows, :] = data
    keep_out[rows:, :] = pick_rows((row,), EXTRA, row.shape[1])


def divide_kernel(*refs):
    coef = refs[-1]
    data, row = add_parts(refs[:-1])
    total = row + 1.0 / prior_var
    for b in range(coef.shape[0] // LANES):
        at = slice(b * LANES, (b + 1) * LANES)
        column = row_to_column(total[:, at])[:, 0:1]
        coef[at, :] = (data[at] / column).astype(BF16)


def in_vmem(value):
    return pltpu.with_memory_space_constraint(value, pltpu.VMEM)


def in_hbm(value):
    return pltpu.with_memory_space_constraint(value, pltpu.HBM)


def vmem_call(kernel, outs, *args, scratch=()):
    vmem = pl.BlockSpec(memory_space=pltpu.VMEM)
    return pl.pallas_call(
        kernel,
        in_specs=[vmem] * len(args),
        out_specs=[vmem] * len(outs),
        out_shape=[pltpu.VMEM(s, d) for s, d in outs],
        scratch_shapes=list(scratch),
        compiler_params=pltpu.CompilerParams(vmem_limit_bytes=VMEM_LIMIT),
    )(*[in_vmem(a) for a in args])


def make_field_kernel(places):
    def kernel(basis, clim, *refs):
        coefs = refs[: len(places)]
        out, buf, sem = refs[-3:]
        here = place()
        block = out.shape[0] // 8
        copies = []
        at = 0
        for i, (coef, (flips, offset)) in enumerate(zip(coefs, places)):
            rows = coef.shape[0]
            acc = jnp.dot(coef[...], basis[...], preferred_element_type=F32)
            buf[at : at + rows, :] = (acc + clim[...]).astype(BF16)
            bx, bc, by = [1 - h if f else h for h, f in zip(here, flips)]
            start = pl.multiple_of((bx * 4 + bc * 2 + by) * block + offset, rows)
            copy = pltpu.make_async_copy(buf.at[pl.ds(at, rows)], out.at[pl.ds(start, rows)], sem.at[i])
            copy.start()
            copies.append(copy)
            at += rows
        for copy in copies:
            copy.wait()

    return kernel


def field_rows(parts, basis, clim, tests, out=None):
    vmem = pl.BlockSpec(memory_space=pltpu.VMEM)
    hbm = pl.BlockSpec(memory_space=pl.ANY)
    cells = basis.shape[1]
    rows = sum(c.shape[0] for c, _, _ in parts)
    args = [in_vmem(v) for v in [basis, clim] + [c for c, _, _ in parts]]
    specs = [vmem] * len(args)
    alias = {}
    if out is not None:
        alias = {len(args): 0}
        args.append(out)
        specs.append(hbm)
    return pl.pallas_call(
        make_field_kernel([(flips, offset) for _, flips, offset in parts]),
        in_specs=specs,
        out_specs=hbm,
        out_shape=jax.ShapeDtypeStruct((tests, cells), BF16),
        input_output_aliases=alias,
        scratch_shapes=[pltpu.VMEM((rows, cells), BF16), pltpu.SemaphoreType.DMA((len(parts),))],
        compiler_params=pltpu.CompilerParams(vmem_limit_bytes=VMEM_LIMIT),
        cost_estimate=pl.CostEstimate(
            flops=2 * rows * basis.shape[0] * cells, transcendentals=0, bytes_accessed=2 * rows * cells
        ),
        name="field",
    )(*args)


def solution(mesh):
    n_group, n_expert = mesh.shape["group"], mesh.shape["expert"]
    assert n_group & (n_group - 1) == 0 and n_expert & (n_expert - 1) == 0
    assert n_group >= 2 and n_expert >= 4

    def swap(value, group_mask, expert_mask):
        pairs = []
        for g in range(n_group):
            for e in range(n_expert):
                pairs.append((g * n_expert + e, (g ^ group_mask) * n_expert + (e ^ expert_mask)))
        return lax.ppermute(value, AXES, pairs)

    def both_masks(a, b):
        return a[0] ^ b[0], a[1] ^ b[1]

    core = (0, 1)
    far = (0, 2)
    near = (1, 0)
    adding = []
    for bit in range(2, n_expert.bit_length() - 1):
        adding.append((0, 1 << bit))
    for bit in range(1, n_group.bit_length() - 1):
        adding.append(((1 << (bit + 1)) - 2, 0))

    def work(train_inputs, inv_factor, weights, candidates, test_ids, basis, climatology):
        tests = test_ids.shape[0]
        out = weights.shape[2]
        block = tests // 8
        assert block == LANES
        ids = test_ids.reshape(tests // LANES, 1, LANES)
        small = (block + EXTRA, out)

        send, keep, *parts = far_half(ids, candidates, train_inputs, inv_factor, weights)
        got = swap(send, *core)
        leaving = vmem_call(leave_kernel, [(small, BF16)] * len(LEAVING), keep, got)
        got_d = swap(leaving[0], *both_masks(far, near))
        got_x = swap(leaving[1], *far)
        got_y = swap(leaving[2], *near)
        send, keep = near_half(ids, candidates, *parts)
        got = swap(send, *core)
        parts = [keep, got, got_x, got_y, got_d]
        for mask in adding:
            send, keep = vmem_call(both_kernel, [(small, BF16), (small, F32)], *parts)
            parts = [keep, swap(send, *mask)]
        (coef,) = vmem_call(divide_kernel, [((block, out), BF16)], *parts)

        clim = climatology.reshape(1, -1)
        by_d = swap(coef, *both_masks(far, near))
        by_x = swap(coef, *far)
        by_y = swap(coef, *near)
        by_c = swap(coef, *core)
        field = field_rows([(coef, (0, 0, 0), 0), (by_c, (0, 1, 0), 0)], basis, clim, tests)
        by_cx = swap(by_x, *core)
        by_cy = swap(by_y, *core)
        field = field_rows([(by_x, (1, 0, 0), 0), (by_y, (0, 0, 1), 0)], basis, clim, tests, field)
        by_cd = swap(by_d, *core)
        parts = [(by_cx, (1, 1, 0), 0), (by_cy, (0, 1, 1), 0), (by_d, (1, 0, 1), 0)]
        field = field_rows(parts, basis, clim, tests, field)
        return field_rows([(by_cd, (1, 1, 1), 0)], basis, clim, tests, field)

    return jax.shard_map(
        work,
        mesh=mesh,
        in_specs=(
            P(AXES, None, None),
            P(AXES, None, None),
            P(AXES, None, None),
            P(),
            P(),
            P(None, AXES),
            P(AXES),
        ),
        out_specs=P(None, AXES),
        check_vma=False,
    )
```
